256 devices in a mesh: row: 8 (over y, core), col: 32 (over x, z).
Axes of the slice: x: 4, y: 4, z: 8, core: 2. Of those that a mesh axis runs over, the one named last changes fastest.
Arguments:
- tokens: bfloat16 [2048, 6144], P('row', 'col'), may hold values from -6 to 6
- cotangent: bfloat16 [2048, 6144], P('row', 'col'), may hold values from -6 to 6
- w_expand: bfloat16 [6144, 12288], P('row', 'col'), may hold values from -0.078125 to 0.078125
- w_reduce: bfloat16 [6144, 12288], P('row', 'col'), may hold values from -0.0546875 to 0.0546875
- expand_mean: bfloat16 [6144, 12288], P('row', 'col'), may hold values from -1 to 1
- expand_mean_scale: float32 [24, 12288], P('row', 'col'), may hold values from 4 to 16
- expand_var: bfloat16 [6144, 12288], P('row', 'col'), may hold values from 0.049804688 to 1
- expand_var_scale: float32 [24, 12288], P('row', 'col'), may hold values from 4 to 16
- reduce_mean: bfloat16 [6144, 12288], P('row', 'col'), may hold values from -1 to 1
- reduce_mean_scale: float32 [24, 12288], P('row', 'col'), may hold values from 4 to 16
- reduce_var: bfloat16 [6144, 12288], P('row', 'col'), may hold values from 0.049804688 to 1
- reduce_var_scale: float32 [24, 12288], P('row', 'col'), may hold values from 4 to 16
Outputs:
- grad_tokens: bfloat16 [2048, 6144], P('row', 'col')
- new_expand: bfloat16 [6144, 12288], P('row', 'col')
- expand_mean_next: bfloat16 [6144, 12288], P('row', 'col')
- expand_mean_scale_next: float32 [24, 12288], P('row', 'col')
- expand_var_next: bfloat16 [6144, 12288], P('row', 'col')
- expand_var_scale_next: float32 [24, 12288], P('row', 'col')
- new_reduce: bfloat16 [6144, 12288], P('row', 'col')
- reduce_mean_next: bfloat16 [6144, 12288], P('row', 'col')
- reduce_mean_scale_next: float32 [24, 12288], P('row', 'col')
- reduce_var_next: bfloat16 [6144, 12288], P('row', 'col')
- reduce_var_scale_next: float32 [24, 12288], P('row', 'col')
The draws below stay inside these ranges and needn't reach their ends.
All inputs are finite; a program needn't handle non-finite values.
Results may differ from the reference program's by a relative error of at most 0.0049.
Values may be sent and summed in bfloat16 or wider, within the bound.
No kernel may reach another device: no remote copies, remote signals or barrier semaphores. Data moves between devices by JAX's collectives and lax.ppermute only.
A program may use at most 128 MiB of HBM per device.

```python
import math
import jax
import jax.numpy as jnp
from jax import lax

D = 6144
FF = 12288
STEP = 10
TOKENS = 2048
NBLK = 24


def block_levels(key, dims, pieces, low, top_value):
    level = 1.0
    for position, parts in pieces:
        draws = jax.random.uniform(jax.random.fold_in(jax.random.fold_in(key, 6), position), (parts,), jnp.float32, low / len(pieces), top_value / len(pieces))
        level = level * jnp.repeat(jnp.exp(draws), dims[position] // parts).reshape((-1,) + (1,) * (len(dims) - 1 - position))
    return level


def gaussian(rng, shape, scale, bound, split=(), dtype=jnp.bfloat16):
    values = scale * jax.random.normal(rng, shape, jnp.float32)
    if split:
        values = values * block_levels(rng, shape, split, -0.22, 0.18)
    return jnp.clip(values, -bound, bound).astype(dtype)


def setup_inputs(seed: int = 0) -> dict:
    seeds = jax.random.split(jax.random.key(seed), 13)
    tokens = gaussian(seeds[0], (TOKENS, D), 1.0, 6.0, ((0, 8), (1, 32)))
    cotangent = gaussian(seeds[1], (TOKENS, D), 1.0, 6.0, ((0, 8), (1, 32)))
    w_expand = gaussian(seeds[2], (D, FF), D ** -0.5, 0.078125, ((0, 8), (1, 32)))
    w_reduce = gaussian(seeds[3], (D, FF), FF ** -0.5, 0.0546875, ((0, 8), (1, 32)))
    expand_mean = jnp.clip(jax.random.uniform(seeds[4], (D, FF), jnp.float32, -1.0, 1.0) * block_levels(seeds[4], (D, FF), ((0, 8), (1, 32)), -0.4, 0.0), -1.0, 1.0).astype(jnp.bfloat16)
    expand_mean_scale = jnp.clip(jnp.exp(math.log(16.0) - 1.3862944 * jax.random.uniform(seeds[5], (NBLK, FF), jnp.float32) ** block_levels(seeds[5], (NBLK, FF), ((0, 8), (1, 32)), -0.2, 0.2)), 4.0, 16.0)
    expand_var = jnp.clip(0.049804688 + 0.9501953 * jax.random.uniform(seeds[6], (D, FF), jnp.float32) ** block_levels(seeds[6], (D, FF), ((0, 8), (1, 32)), -0.2, 0.2), 0.049804688, 1.0).astype(jnp.bfloat16)
    expand_var_scale = jnp.clip(jnp.exp(math.log(16.0) - 1.3862944 * jax.random.uniform(seeds[7], (NBLK, FF), jnp.float32) ** block_levels(seeds[7], (NBLK, FF), ((0, 8), (1, 32)), -0.2, 0.2)), 4.0, 16.0)
    reduce_mean = jnp.clip(jax.random.uniform(seeds[8], (D, FF), jnp.float32, -1.0, 1.0) * block_levels(seeds[8], (D, FF), ((0, 8), (1, 32)), -0.4, 0.0), -1.0, 1.0).astype(jnp.bfloat16)
    reduce_mean_scale = jnp.clip(jnp.exp(math.log(16.0) - 1.3862944 * jax.random.uniform(seeds[9], (NBLK, FF), jnp.float32) ** block_levels(seeds[9], (NBLK, FF), ((0, 8), (1, 32)), -0.2, 0.2)), 4.0, 16.0)
    reduce_var = jnp.clip(0.049804688 + 0.9501953 * jax.random.uniform(seeds[10], (D, FF), jnp.float32) ** block_levels(seeds[10], (D, FF), ((0, 8), (1, 32)), -0.2, 0.2), 0.049804688, 1.0).astype(jnp.bfloat16)
    reduce_var_scale = jnp.clip(jnp.exp(math.log(16.0) - 1.3862944 * jax.random.uniform(seeds[11], (NBLK, FF), jnp.float32) ** block_levels(seeds[11], (NBLK, FF), ((0, 8), (1, 32)), -0.2, 0.2)), 4.0, 16.0)
    return {"tokens": tokens, "cotangent": cotangent, "w_expand": w_expand, "w_reduce": w_reduce, "expand_mean": expand_mean, "expand_mean_scale": expand_mean_scale, "expand_var": expand_var, "expand_var_scale": expand_var_scale, "reduce_mean": reduce_mean, "reduce_mean_scale": reduce_mean_scale, "reduce_var": reduce_var, "reduce_var_scale": reduce_var_scale}


beta_one = 0.9
beta_two = 0.999
adam_eps = 1e-08
learn_rate = 0.001
decay_rate = 0.1
scale_eps = 1e-06

def gelu_pair(pre_act):
    cdf_part = 0.5 * (1.0 + lax.erf(pre_act * 0.7071067811865476))
    slope = cdf_part + pre_act * jnp.exp(-0.5 * pre_act * pre_act) * 0.3989422804014327
    return (pre_act * cdf_part, slope)

def spread_scale(values, scale):
    blocks = scale.shape[0]
    shaped = values.reshape(blocks, values.shape[0] // blocks, values.shape[1])
    return (shaped * scale[:, None, :]).reshape(values.shape)

def block_max(values, blocks):
    shaped = values.reshape(blocks, values.shape[0] // blocks, values.shape[1])
    return lax.optimization_barrier(jnp.max(jnp.abs(shaped), axis=1)) + scale_eps

def adam_step(weight, grad_w, mean_q, mean_scale, var_q, var_scale):
    blocks = mean_scale.shape[0]
    mean_new = beta_one * spread_scale(mean_q.astype(jnp.float32), mean_scale) + (1.0 - beta_one) * grad_w
    var_new = beta_two * spread_scale(var_q.astype(jnp.float32), var_scale) + (1.0 - beta_two) * grad_w * grad_w
    mean_hat = mean_new / (1.0 - beta_one ** STEP)
    var_hat = var_new / (1.0 - beta_two ** STEP)
    old_weight = weight.astype(jnp.float32)
    new_weight = (old_weight - learn_rate * (mean_hat / (jnp.sqrt(var_hat) + adam_eps) + decay_rate * old_weight)).astype(jnp.bfloat16)
    mean_scale_next = block_max(mean_new, blocks)
    var_scale_next = block_max(var_new, blocks)
    mean_next = spread_scale(mean_new, 1.0 / mean_scale_next).astype(jnp.bfloat16)
    var_next = spread_scale(var_new, 1.0 / var_scale_next).astype(jnp.bfloat16)
    return (new_weight, mean_next, mean_scale_next, var_next, var_scale_next)

def reference(tokens, cotangent, w_expand, w_reduce, expand_mean, expand_mean_scale, expand_var, expand_var_scale, reduce_mean, reduce_mean_scale, reduce_var, reduce_var_scale):
    pre_act = jnp.dot(tokens, w_expand, preferred_element_type=jnp.float32)
    activated, slope = gelu_pair(pre_act)
    activated = activated.astype(jnp.bfloat16)
    act_grad = jnp.dot(cotangent, w_reduce, preferred_element_type=jnp.float32)
    pre_grad = (act_grad * slope).astype(jnp.bfloat16)
    grad_tokens = jnp.dot(pre_grad, w_expand.T, preferred_element_type=jnp.float32).astype(jnp.bfloat16)
    grad_expand = jnp.dot(tokens.T, pre_grad, preferred_element_type=jnp.float32)
    grad_reduce = jnp.dot(cotangent.T, activated, preferred_element_type=jnp.float32)
    first = adam_step(w_expand, grad_expand, expand_mean, expand_mean_scale, expand_var, expand_var_scale)
    second = adam_step(w_reduce, grad_reduce, reduce_mean, reduce_mean_scale, reduce_var, reduce_var_scale)
    return (grad_tokens, first[0], first[1], first[2], first[3], first[4], second[0], second[1], second[2], second[3], second[4])
```

```python
import jax
import jax.numpy as jnp
from jax import lax
from jax.experimental import pallas as pl
from jax.experimental.pallas import tpu as pltpu
from jax.sharding import Mesh, PartitionSpec as P

STEP = 10

beta_one = 0.9
beta_two = 0.999
adam_eps = 1e-08
learn_rate = 0.001
decay_rate = 0.1
scale_eps = 1e-06

NY, NC, NX, NZ = 4, 2, 4, 8
ZL = 4
AXES = ("y", "core", "x", "z")
DZ = (0, 1, 7, 2, 6, 3, 5, 4)
DX = (0, 1, 3, 2)


f32 = jnp.float32
bf16 = jnp.bfloat16


def gelu_pair(pre_act):
    cdf_part = 0.5 * (1.0 + lax.erf(pre_act * 0.7071067811865476))
    slope = cdf_part + pre_act * jnp.exp(-0.5 * pre_act * pre_act) * 0.3989422804014327
    return (pre_act * cdf_part, slope)


def ring(n, k):
    return [(i, (i + k) % n) for i in range(n)]


def flat(y, core, x, z):
    return ((y * NC + core) * NX + x) * NZ + z


def swap_perm(s):
    perm = []
    for y in range(NY):
        for core in range(NC):
            for x in range(NX):
                for z in range(NZ):
                    half, low = z // ZL, z % ZL
                    perm.append(
                        (flat(y, core, x, z), flat(x, half, y, core * ZL + (low + s) % ZL))
                    )
    return perm


def adam_kernel(x_ref, g_ref, w_ref, m_ref, ms_ref, v_ref, vs_ref,
                wn_ref, mn_ref, msn_ref, vn_ref, vsn_ref):
    i = pl.program_id(0)
    grad = lax.dot_general(
        x_ref[...], g_ref[...], (((0,), (0,)), ((), ())), preferred_element_type=f32
    )
    ms = ms_ref[pl.ds(i, 1), :]
    vs = vs_ref[pl.ds(i, 1), :]
    mean = beta_one * (m_ref[...].astype(f32) * ms) + (1.0 - beta_one) * grad
    var = beta_two * (v_ref[...].astype(f32) * vs) + (1.0 - beta_two) * grad * grad
    mean_hat = mean / (1.0 - beta_one**STEP)
    var_hat = var / (1.0 - beta_two**STEP)
    old = w_ref[...].astype(f32)
    new = old - learn_rate * (mean_hat / (jnp.sqrt(var_hat) + adam_eps) + decay_rate * old)
    wn_ref[...] = new.astype(bf16)
    ms_next = jnp.max(jnp.abs(mean), axis=0, keepdims=True) + scale_eps
    vs_next = jnp.max(jnp.abs(var), axis=0, keepdims=True) + scale_eps
    msn_ref[pl.ds(i, 1), :] = ms_next
    vsn_ref[pl.ds(i, 1), :] = vs_next
    mn_ref[...] = (mean * (1.0 / ms_next)).astype(bf16)
    vn_ref[...] = (var * (1.0 / vs_next)).astype(bf16)


def adam_step(slab, hidden, weight, mean_q, mean_scale, var_q, var_scale):
    rows, cols = weight.shape
    blocks = mean_scale.shape[0]
    size = rows // blocks
    tokens = slab.shape[0]
    tile = pl.BlockSpec((size, cols), lambda i: (i, 0))
    scale = pl.BlockSpec((blocks, cols), lambda i: (0, 0))
    return pl.pallas_call(
        adam_kernel,
        grid=(blocks,),
        in_specs=[
            pl.BlockSpec((tokens, size), lambda i: (0, i)),
            pl.BlockSpec((tokens, cols), lambda i: (0, 0)),
            tile, tile, scale, tile, scale,
        ],
        out_specs=(tile, tile, scale, tile, scale),
        out_shape=(
            jax.ShapeDtypeStruct((rows, cols), bf16),
            jax.ShapeDtypeStruct((rows, cols), bf16),
            jax.ShapeDtypeStruct((blocks, cols), f32),
            jax.ShapeDtypeStruct((rows, cols), bf16),
            jax.ShapeDtypeStruct((blocks, cols), f32),
        ),
        cost_estimate=pl.CostEstimate(
            flops=2 * tokens * rows * cols,
            transcendentals=2 * rows * cols,
            bytes_accessed=2 * tokens * (rows + cols) + 12 * rows * cols,
        ),
        name="adam",
    )(slab, hidden, weight, mean_q, mean_scale, var_q, var_scale)


def local(
    tokens,
    cotangent,
    w_expand,
    w_reduce,
    expand_mean,
    expand_mean_scale,
    expand_var,
    expand_var_scale,
    reduce_mean,
    reduce_mean_scale,
    reduce_var,
    reduce_var_scale,
):
    core = lax.axis_index("core")
    low = lax.axis_index("z") % ZL
    tl, fl = tokens.shape
    piece = tl // ZL
    width = fl * ZL
    hid = w_expand.shape[1]
    count = tl * NY * NC

    def along_x(v, k):
        return lax.ppermute(v, "x", ring(NX, k))

    def along_z(v, k):
        return lax.ppermute(v, "z", ring(NZ, k))

    both = jnp.concatenate([tokens, cotangent], axis=1).reshape(ZL, piece, 2 * fl)
    got = jnp.stack(
        [
            lax.ppermute(
                lax.dynamic_index_in_dim(both, (low + s) % ZL, 0, keepdims=False),
                AXES,
                swap_perm(s),
            )
            for s in range(ZL)
        ]
    )
    parts = [
        lax.dynamic_index_in_dim(got, (low - f) % ZL, 0, keepdims=False) for f in range(ZL)
    ]
    tok_piece = jnp.concatenate([p[:, :fl] for p in parts], axis=1)
    cot_piece = jnp.concatenate([p[:, fl:] for p in parts], axis=1)

    tok_x = jnp.concatenate(
        [tok_piece, along_x(tok_piece, 1), along_x(tok_piece, 3), along_x(tok_piece, 2)]
    )
    up1, dn1 = along_z(tok_x, 1), along_z(tok_x, -1)
    cot_z = jnp.concatenate([cot_piece] + [along_z(cot_piece, k) for k in DZ[1:]])
    up2, dn2 = along_z(up1, 1), along_z(dn1, -1)
    up3, dn3 = along_z(up2, 1), along_z(dn2, -1)
    half = tok_x.shape[0] // 2
    far = [along_z(up3[:half], 1), along_z(dn3[half:], -1)]
    slab = jnp.concatenate([tok_x, up1, dn1, up2, dn2, up3, dn3] + far)

    cx1, cx3 = along_x(cot_z, 1), along_x(cot_z, -1)
    half = cot_z.shape[0] // 2
    cx2 = jnp.concatenate([along_x(cx1[:half], 1), along_x(cx3[half:], -1)])
    cot_slab = jnp.stack(
        [v.reshape(NZ, piece, width) for v in (cot_z, cx1, cx3, cx2)], axis=1
    ).reshape(count, width)

    def over_core(part):
        own = lax.dynamic_slice_in_dim(part, core * (count // 2), count // 2)
        other = lax.dynamic_slice_in_dim(part, (1 - core) * (count // 2), count // 2)
        return own + lax.ppermute(other, "core", ring(NC, 1))

    pre_part = over_core(jnp.dot(slab, w_expand, preferred_element_type=f32))
    act_part = over_core(jnp.dot(cot_slab, w_reduce, preferred_element_type=f32))
    row_part = jnp.concatenate([pre_part, act_part], axis=1).reshape(NY, tl, 2 * hid)
    here = lax.axis_index("y")
    mine = lax.dynamic_index_in_dim(row_part, here, 0, keepdims=False)
    sent = lax.all_to_all(row_part.astype(bf16), "y", 0, 0)
    sums = mine
    for k in range(1, NY):
        sums = sums + lax.dynamic_index_in_dim(sent, (here + k) % NY, 0, keepdims=False).astype(f32)
    activated, slope = gelu_pair(sums[:, :hid])
    activated = activated.astype(bf16)
    pre_grad = (sums[:, hid:] * slope).astype(bf16)

    def over_row(v):
        four = lax.all_to_all(
            jnp.broadcast_to(v[None], (NY,) + v.shape), "y", 0, 0
        ).reshape(count // 2, hid)
        other = lax.ppermute(four, "core", ring(NC, 1))
        return jnp.concatenate(
            [jnp.where(core == 0, four, other), jnp.where(core == 0, other, four)]
        )

    pre_grad = over_row(pre_grad)
    pre_grad, activated = lax.optimization_barrier((pre_grad, activated))
    activated = over_row(activated)

    grad_part = lax.dot_general(
        pre_grad, w_expand, (((1,), (1,)), ((), ())), preferred_element_type=f32
    ).astype(bf16).reshape(NZ, NX, piece, width)
    cut = (width // 3) * 2
    first, second = grad_part[..., :cut], grad_part[..., cut:]

    def add(own, others):
        total = own.astype(f32)
        for v in others:
            total = total + v.astype(f32)
        return total

    in_x = [along_x(first[:, j], -DX[j]) for j in range(1, NX)]
    in_z = [along_z(second[i], -DZ[i]) for i in range(1, NZ)]
    new_expand = adam_step(
        slab, pre_grad, w_expand, expand_mean, expand_mean_scale, expand_var, expand_var_scale
    )
    in_x, in_z, new_expand = lax.optimization_barrier((in_x, in_z, new_expand))
    first = add(first[:, 0], in_x).astype(bf16)
    second = add(second[0], in_z).astype(bf16)
    in_z = [along_z(first[i], -DZ[i]) for i in range(1, NZ)]
    in_x = [along_x(second[j], -DX[j]) for j in range(1, NX)]
    new_reduce = adam_step(
        cot_slab, activated, w_reduce, reduce_mean, reduce_mean_scale, reduce_var, reduce_var_scale
    )
    in_x, in_z, new_reduce = lax.optimization_barrier((in_x, in_z, new_reduce))
    first = add(first[0], in_z).astype(bf16)
    second = add(second[0], in_x).astype(bf16)
    grad_piece = jnp.concatenate([first, second], axis=1)
    grad_piece = jnp.stack([grad_piece[:, f * fl : (f + 1) * fl] for f in range(ZL)])
    back = jnp.stack(
        [
            lax.ppermute(
                lax.dynamic_index_in_dim(grad_piece, (low - s) % ZL, 0, keepdims=False),
                AXES,
                [(d, o) for o, d in swap_perm(s)],
            )
            for s in range(ZL)
        ]
    )
    grad_tokens = jnp.concatenate(
        [lax.dynamic_index_in_dim(back, (t - low) % ZL, 0, keepdims=False) for t in range(ZL)]
    )

    return (grad_tokens,) + tuple(new_expand) + tuple(new_reduce)


def solution(mesh):
    four = Mesh(mesh.devices.reshape(NY, NC, NX, NZ), AXES)
    spec = P(("y", "core"), ("x", "z"))
    return jax.shard_map(
        local, mesh=four, in_specs=(spec,) * 12, out_specs=(spec,) * 11, check_vma=False
    )
```

```python
import jax
import jax.numpy as jnp
from jax import lax
from jax.experimental import pallas as pl
from jax.experimental.pallas import tpu as pltpu
from jax.sharding import Mesh, PartitionSpec as P


STEP = 10

beta_one = 0.9
beta_two = 0.999
adam_eps = 1e-08
learn_rate = 0.001
decay_rate = 0.1
scale_eps = 1e-06

NY, NC, NX, NZ = 4, 2, 4, 8
ZL = 4
AXES = ("y", "core", "x", "z")
DX = (0, 1, 3, 2)


f32 = jnp.float32
bf16 = jnp.bfloat16


def gelu_pair(pre_act):
    cdf_part = 0.5 * (1.0 + lax.erf(pre_act * 0.7071067811865476))
    slope = cdf_part + pre_act * jnp.exp(-0.5 * pre_act * pre_act) * 0.3989422804014327
    return (pre_act * cdf_part, slope)


def ring(n, k):
    return [(i, (i + k) % n) for i in range(n)]


def flat(y, core, x, z):
    return ((y * NC + core) * NX + x) * NZ + z


def swap_perm():
    perm = []
    for y in range(NY):
        for core in range(NC):
            for x in range(NX):
                for z in range(NZ):
                    half, low = z // ZL, z % ZL
                    perm.append((flat(y, core, x, z), flat(x, half, y, core * ZL + low)))
    return perm


def pick(v, i):
    return lax.dynamic_index_in_dim(v, i, 0, keepdims=False)


def along(axis, n, v, k):
    return lax.ppermute(v, axis, ring(n, k))


def step(axis, n, up, down):
    return along(axis, n, up, 1), along(axis, n, down, -1)


def farthest(axis, n, up, down):
    half = up.shape[0] // 2
    return jnp.concatenate([along(axis, n, up[:half], 1), along(axis, n, down[half:], -1)])


def place(here, n, chunks):
    first = chunks[0][1]
    whole = jnp.zeros((n,) + first.shape, first.dtype)
    for k, v in chunks:
        whole = lax.dynamic_update_index_in_dim(whole, v, (here - k) % n, 0)
    return whole


def adam_kernel(x_ref, g_ref, w_ref, m_ref, ms_ref, v_ref, vs_ref,
                wn_ref, mn_ref, msn_ref, vn_ref, vsn_ref):
    i = pl.program_id(0)
    grad = sum(
        jnp.dot(x_ref[h], g_ref[h], preferred_element_type=f32) for h in range(NC)
    )
    ms = ms_ref[pl.ds(i, 1), :]
    vs = vs_ref[pl.ds(i, 1), :]
    mean = beta_one * (m_ref[...].astype(f32) * ms) + (1.0 - beta_one) * grad
    var = beta_two * (v_ref[...].astype(f32) * vs) + (1.0 - beta_two) * grad * grad
    mean_hat = mean / (1.0 - beta_one**STEP)
    var_hat = var / (1.0 - beta_two**STEP)
    old = w_ref[...].astype(f32)
    new = old - learn_rate * (mean_hat / (jnp.sqrt(var_hat) + adam_eps) + decay_rate * old)
    wn_ref[...] = new.astype(bf16)
    ms_next = jnp.max(jnp.abs(mean), axis=0, keepdims=True) + scale_eps
    vs_next = jnp.max(jnp.abs(var), axis=0, keepdims=True) + scale_eps
    msn_ref[pl.ds(i, 1), :] = ms_next
    vsn_ref[pl.ds(i, 1), :] = vs_next
    mn_ref[...] = (mean * (1.0 / ms_next)).astype(bf16)
    vn_ref[...] = (var * (1.0 / vs_next)).astype(bf16)


def adam_step(slab, hidden, weight, mean_q, mean_scale, var_q, var_scale):
    rows, cols = weight.shape
    blocks = mean_scale.shape[0]
    size = rows // blocks
    tokens = slab.shape[2]
    tile = pl.BlockSpec((size, cols), lambda i: (i, 0))
    scale = pl.BlockSpec((blocks, cols), lambda i: (0, 0))
    return pl.pallas_call(
        adam_kernel,
        grid=(blocks,),
        in_specs=[
            pl.BlockSpec((NC, size, tokens), lambda i: (0, i, 0)),
            pl.BlockSpec((NC, tokens, cols), lambda i: (0, 0, 0)),
            tile, tile, scale, tile, scale,
        ],
        out_specs=(tile, tile, scale, tile, scale),
        out_shape=(
            jax.ShapeDtypeStruct((rows, cols), bf16),
            jax.ShapeDtypeStruct((rows, cols), bf16),
            jax.ShapeDtypeStruct((blocks, cols), f32),
            jax.ShapeDtypeStruct((rows, cols), bf16),
            jax.ShapeDtypeStruct((blocks, cols), f32),
        ),
        cost_estimate=pl.CostEstimate(
            flops=2 * NC * tokens * rows * cols,
            transcendentals=2 * rows * cols,
            bytes_accessed=2 * NC * tokens * (rows + cols) + 12 * rows * cols,
        ),
        compiler_params=pltpu.CompilerParams(vmem_limit_bytes=24 * 1024 * 1024),
        name="adam",
    )(slab, hidden, weight, mean_q, mean_scale, var_q, var_scale)


def local(
    tokens,
    cotangent,
    w_expand,
    w_reduce,
    expand_mean,
    expand_mean_scale,
    expand_var,
    expand_var_scale,
    reduce_mean,
    reduce_mean_scale,
    reduce_var,
    reduce_var_scale,
):
    y, core, z = (lax.axis_index(a) for a in ("y", "core", "z"))
    tl, fl = tokens.shape
    width = fl * ZL
    hid = w_expand.shape[1]

    got = lax.ppermute(jnp.concatenate([tokens.T, cotangent.T]), AXES, swap_perm())
    tok_piece, cot_piece = got[:fl], got[fl:]

    hold = lax.optimization_barrier

    def gather(axis, n, v):
        return lax.all_to_all(jnp.broadcast_to(v[None], (n,) + v.shape), axis, 0, 0)

    cut = (fl // 4) * 3
    by_block = w_expand.reshape(ZL, fl, hid)
    w_first = by_block[:, :cut].reshape(ZL * cut, hid)
    w_second = by_block[:, cut:].reshape(ZL * (fl - cut), hid)

    cot_z = gather("z", NZ, cot_piece)
    tok_x = jnp.concatenate([tok_piece] + [along("x", NX, tok_piece, k) for k in DX[1:]], axis=1)
    ta = step("z", NZ, tok_x, tok_x)
    ta, cot_z, w_first, w_second = hold((ta, cot_z, w_first, w_second))
    xa = step("x", NX, cot_z, cot_z)
    tb = step("z", NZ, *ta)
    tc = step("z", NZ, *tb)
    tc, xa = hold((tc, xa))
    xb = farthest("x", NX, *xa)
    td = farthest("z", NZ, *tc)
    slab = place(
        z, NZ, [(0, tok_x), (1, ta[0]), (7, ta[1]), (2, tb[0]), (6, tb[1]),
                (3, tc[0]), (5, tc[1]), (4, td)],
    ).reshape(NC, width, NX * tl)

    def part(slab, weight, h):
        return lax.dot_general(
            pick(slab, h), weight, (((0,), (0,)), ((), ())), preferred_element_type=f32
        )

    def over_core(slab, weight):
        other = along("core", NC, part(slab, weight, 1 - core), 1)
        return part(slab, weight, core) + other

    def halves(chunks):
        return jnp.concatenate(chunks, axis=2).reshape(NC, width, -1)

    pre_part = over_core(slab, w_expand).reshape(NY, tl, hid)
    early = over_core(halves([cot_z, xa[0], xa[1]]), w_reduce)
    late = over_core(halves([xb]), w_reduce)
    act_part = jnp.concatenate([early, late]).reshape(NY, tl, hid)
    cot_slab = halves([cot_z, xa[0], xa[1], xb])

    def chunk(i):
        return jnp.concatenate([pick(pre_part, i), pick(act_part, i)])

    sums = chunk(y)
    for k in (1, 3, 2):
        sums = sums + along("y", NY, chunk((y + k) % NY).astype(bf16), k).astype(f32)
    activated, slope = gelu_pair(sums[:tl])
    activated = activated.astype(bf16)
    pre_grad = (sums[tl:] * slope).astype(bf16)

    def to_row(half):
        half = half.reshape(NY * tl, hid)
        return place(core, NC, [(0, half), (1, along("core", NC, half, 1))])

    pre_grad = to_row(gather("y", NY, pre_grad))

    by_x = pre_grad.reshape(NC, NX, tl, hid)

    def times(weight, grad):
        return lax.dot_general(
            weight, grad, (((1,), (1,)), ((), ())), preferred_element_type=f32
        )

    def add(own, others):
        total = own
        for v in others:
            total = total + v.astype(f32)
        return total

    def first_part(j):
        return times(w_first, by_x[:, j].reshape(NC * tl, hid))

    def by_z(v, size):
        cols = v.shape[1] // NC
        return jnp.stack([v[:, h * cols : (h + 1) * cols] for h in range(NC)]).reshape(
            NZ, size, cols
        )

    in_x = [along("x", NX, first_part(j).astype(bf16), -DX[j]) for j in range(1, NX)]
    second = by_z(times(w_second, pre_grad.reshape(-1, hid)).astype(bf16), fl - cut)
    second, activated = hold((second, activated))
    in_z = lax.all_to_all(second, "z", 0, 0)
    others = [(k, along("y", NY, activated, k)) for k in (1, 3, 2)]
    activated = to_row(place(y, NY, [(0, activated)] + others))
    first = first_part(0)
    new_expand = adam_step(
        slab, pre_grad, w_expand, expand_mean, expand_mean_scale, expand_var, expand_var_scale
    )
    in_x, in_z, new_expand = hold((in_x, in_z, new_expand))
    first = by_z(add(first, in_x), cut)
    in_z_first = lax.all_to_all(first.astype(bf16), "z", 0, 0)
    second = jnp.sum(in_z.astype(f32), axis=0)
    in_x_second = [
        along("x", NX, second[:, j * tl : (j + 1) * tl].astype(bf16), -DX[j]) for j in range(1, NX)
    ]
    new_reduce = adam_step(
        cot_slab, activated, w_reduce, reduce_mean, reduce_mean_scale, reduce_var, reduce_var_scale
    )
    in_z_first, in_x_second, new_reduce = hold((in_z_first, in_x_second, new_reduce))
    first = add(pick(first, z), [pick(in_z_first, (z + k) % NZ) for k in range(1, NZ)])
    piece = jnp.concatenate([first, add(second[:, :tl], in_x_second)]).astype(bf16)
    grad_tokens = lax.ppermute(piece, AXES, [(d, s) for s, d in swap_perm()]).T
    return (grad_tokens,) + tuple(new_expand) + tuple(new_reduce)


def solution(mesh):
    four = Mesh(mesh.devices.reshape(NY, NC, NX, NZ), AXES)
    spec = P(("y", "core"), ("x", "z"))
    return jax.shard_map(
        local, mesh=four, in_specs=(spec,) * 12, out_specs=(spec,) * 11, check_vma=False
    )
```

```python
import jax
import jax.numpy as jnp
from jax import lax
from jax.experimental.layout import Layout, with_layout_constraint
from jax.experimental import pallas as pl
from jax.experimental.pallas import tpu as pltpu
from jax.sharding import Mesh, PartitionSpec as P


STEP = 10

beta_one = 0.9
beta_two = 0.999
adam_eps = 1e-08
learn_rate = 0.001
decay_rate = 0.1
scale_eps = 1e-06

NY, NC, NX, NZ = 4, 2, 4, 8
ZL = 4
AXES = ("y", "core", "x", "z")
DX = (0, 1, 3, 2)


f32 = jnp.float32
bf16 = jnp.bfloat16


def gelu_pair(pre_act):
    cdf_part = 0.5 * (1.0 + lax.erf(pre_act * 0.7071067811865476))
    slope = cdf_part + pre_act * jnp.exp(-0.5 * pre_act * pre_act) * 0.3989422804014327
    return (pre_act * cdf_part, slope)


def ring(n, k):
    return [(i, (i + k) % n) for i in range(n)]


def flat(y, core, x, z):
    return ((y * NC + core) * NX + x) * NZ + z


def swap_perm():
    perm = []
    for y in range(NY):
        for core in range(NC):
            for x in range(NX):
                for z in range(NZ):
                    half, low = z // ZL, z % ZL
                    perm.append((flat(y, core, x, z), flat(x, half, y, core * ZL + low)))
    return perm


def pick(v, i):
    return lax.dynamic_index_in_dim(v, i, 0, keepdims=False)


def along(axis, n, v, k):
    return lax.ppermute(v, axis, ring(n, k))


def step(axis, n, up, down):
    return along(axis, n, up, 1), along(axis, n, down, -1)


def farthest(axis, n, up, down):
    half = up.shape[0] // 2
    return jnp.concatenate([along(axis, n, up[:half], 1), along(axis, n, down[half:], -1)])


def place(here, n, chunks):
    first = chunks[0][1]
    whole = jnp.zeros((n,) + first.shape, first.dtype)
    for k, v in chunks:
        whole = lax.dynamic_update_index_in_dim(whole, v, (here - k) % n, 0)
    return whole


def adam_kernel(x_ref, g_ref, w_ref, m_ref, ms_ref, v_ref, vs_ref,
                wn_ref, mn_ref, msn_ref, vn_ref, vsn_ref):
    i = pl.program_id(0)
    grad = sum(
        jnp.dot(x_ref[h], g_ref[h], preferred_element_type=f32) for h in range(NC)
    )
    ms = ms_ref[pl.ds(i, 1), :]
    vs = vs_ref[pl.ds(i, 1), :]
    mean = beta_one * (m_ref[...].astype(f32) * ms) + (1.0 - beta_one) * grad
    var = beta_two * (v_ref[...].astype(f32) * vs) + (1.0 - beta_two) * grad * grad
    mean_hat = mean / (1.0 - beta_one**STEP)
    var_hat = var / (1.0 - beta_two**STEP)
    old = w_ref[...].astype(f32)
    new = old - learn_rate * (mean_hat / (jnp.sqrt(var_hat) + adam_eps) + decay_rate * old)
    wn_ref[...] = new.astype(bf16)
    ms_next = jnp.max(jnp.abs(mean), axis=0, keepdims=True) + scale_eps
    vs_next = jnp.max(jnp.abs(var), axis=0, keepdims=True) + scale_eps
    msn_ref[pl.ds(i, 1), :] = ms_next
    vsn_ref[pl.ds(i, 1), :] = vs_next
    mn_ref[...] = (mean * (1.0 / ms_next)).astype(bf16)
    vn_ref[...] = (var * (1.0 / vs_next)).astype(bf16)


def adam_step(slab, hidden, weight, mean_q, mean_scale, var_q, var_scale):
    rows, cols = weight.shape
    blocks = mean_scale.shape[0]
    size = rows // blocks
    tokens = slab.shape[2]
    weight, mean_q, var_q = (
        pltpu.with_memory_space_constraint(v, pltpu.HBM) for v in (weight, mean_q, var_q)
    )
    tile = pl.BlockSpec((size, cols), lambda i: (i, 0))
    scale = pl.BlockSpec((blocks, cols), lambda i: (0, 0))
    return pl.pallas_call(
        adam_kernel,
        grid=(blocks,),
        in_specs=[
            pl.BlockSpec((NC, size, tokens), lambda i: (0, i, 0)),
            pl.BlockSpec((NC, tokens, cols), lambda i: (0, 0, 0)),
            tile, tile, scale, tile, scale,
        ],
        out_specs=(tile, tile, scale, tile, scale),
        out_shape=(
            jax.ShapeDtypeStruct((rows, cols), bf16),
            jax.ShapeDtypeStruct((rows, cols), bf16),
            jax.ShapeDtypeStruct((blocks, cols), f32),
            jax.ShapeDtypeStruct((rows, cols), bf16),
            jax.ShapeDtypeStruct((blocks, cols), f32),
        ),
        cost_estimate=pl.CostEstimate(
            flops=2 * NC * tokens * rows * cols,
            transcendentals=2 * rows * cols,
            bytes_accessed=2 * NC * tokens * (rows + cols) + 12 * rows * cols,
        ),
        compiler_params=pltpu.CompilerParams(vmem_limit_bytes=24 * 1024 * 1024),
        name="adam",
    )(slab, hidden, weight, mean_q, mean_scale, var_q, var_scale)


def local(
    tokens,
    cotangent,
    w_expand,
    w_reduce,
    expand_mean,
    expand_mean_scale,
    expand_var,
    expand_var_scale,
    reduce_mean,
    reduce_mean_scale,
    reduce_var,
    reduce_var_scale,
):
    y, core, z = (lax.axis_index(a) for a in ("y", "core", "z"))
    tl, fl = tokens.shape
    width = fl * ZL
    hid = w_expand.shape[1]

    got = lax.ppermute(jnp.concatenate([tokens.T, cotangent.T]), AXES, swap_perm())
    tok_piece, cot_piece = got[:fl], got[fl:]

    hold = lax.optimization_barrier

    def gather(axis, n, v):
        return lax.all_to_all(jnp.broadcast_to(v[None], (n,) + v.shape), axis, 0, 0)

    cut = (fl // 4) * 3
    by_block = w_expand.reshape(ZL, fl, hid)
    w_first = by_block[:, :cut].reshape(ZL * cut, hid)
    w_second = by_block[:, cut:].reshape(ZL * (fl - cut), hid)

    cot_z = gather("z", NZ, cot_piece)
    tok_x = jnp.concatenate([tok_piece] + [along("x", NX, tok_piece, k) for k in DX[1:]], axis=1)
    ta = step("z", NZ, tok_x, tok_x)
    ta, cot_z, w_first, w_second, wt_expand, wt_reduce = hold(
        (ta, cot_z, w_first, w_second, w_expand.T, w_reduce.T)
    )
    xa = step("x", NX, cot_z, cot_z)
    tb = step("z", NZ, *ta)
    tc = step("z", NZ, *tb)
    tc, xa = hold((tc, xa))
    xb = farthest("x", NX, *xa)
    td = farthest("z", NZ, *tc)
    slab = place(
        z, NZ, [(0, tok_x), (1, ta[0]), (7, ta[1]), (2, tb[0]), (6, tb[1]),
                (3, tc[0]), (5, tc[1]), (4, td)],
    ).reshape(NC, width, NX * tl)

    def part(slab, weight, h):
        return jnp.dot(weight, pick(slab, h), preferred_element_type=f32)

    def over_core(slab, weight):
        other = part(slab, weight, 1 - core)
        other = along("core", NC, other, 1)
        total = part(slab, weight, core) + other
        return jnp.stack([total[:, i : i + tl] for i in range(0, total.shape[1], tl)])

    def halves(chunks):
        return jnp.concatenate(chunks, axis=2).reshape(NC, width, -1)

    pre_part = over_core(slab, wt_expand)
    early = over_core(halves([cot_z, xa[0], xa[1]]), wt_reduce)
    late = over_core(halves([xb]), wt_reduce)
    act_part = jnp.concatenate([early, late])
    cot_slab = halves([cot_z, xa[0], xa[1], xb])

    def over_y(part):
        total = pick(part, y)
        for k in (1, 3, 2):
            total = total + along("y", NY, pick(part, (y + k) % NY).astype(bf16), k).astype(f32)
        return total

    pre_act = over_y(pre_part)
    act_grad = over_y(act_part)
    slope = gelu_pair(pre_act)[1]
    rows = Layout(major_to_minor=(0, 1))
    pre_grad = with_layout_constraint((act_grad * slope).astype(bf16).T, rows)

    def to_row(half):
        half = half.reshape(NY * tl, hid)
        return place(core, NC, [(0, half), (1, along("core", NC, half, 1))])

    pre_grad = to_row(gather("y", NY, pre_grad))

    by_x = pre_grad.reshape(NC, NX, tl, hid)

    def times(weight, grad):
        return lax.dot_general(
            weight, grad, (((1,), (1,)), ((), ())), preferred_element_type=f32
        )

    def add(own, others):
        total = own
        for v in others:
            total = total + v.astype(f32)
        return total

    def first_part(j):
        return times(w_first, by_x[:, j].reshape(NC * tl, hid))

    def by_z(v, size):
        cols = v.shape[1] // NC
        return jnp.stack([v[:, h * cols : (h + 1) * cols] for h in range(NC)]).reshape(
            NZ, size, cols
        )

    sends = [first_part(j).astype(bf16) for j in range(1, NX)]
    in_x = [along("x", NX, v, -d) for v, d in zip(sends, DX[1:])]
    sends, w_second, pre_act = hold((sends, w_second, pre_act))
    activated = with_layout_constraint(gelu_pair(pre_act)[0].astype(bf16).T, rows)
    second = by_z(times(w_second, pre_grad.reshape(-1, hid)).astype(bf16), fl - cut)
    in_z = lax.all_to_all(second, "z", 0, 0)
    others = [(k, along("y", NY, activated, k)) for k in (1, 3, 2)]
    activated = to_row(place(y, NY, [(0, activated)] + others))
    first = first_part(0)
    new_expand = adam_step(
        slab, pre_grad, w_expand, expand_mean, expand_mean_scale, expand_var, expand_var_scale
    )
    in_x, in_z, new_expand = hold((in_x, in_z, new_expand))
    first = by_z(add(first, in_x), cut)
    in_z_first = lax.all_to_all(first.astype(bf16), "z", 0, 0)
    second = jnp.sum(in_z.astype(f32), axis=0)
    in_x_second = [
        along("x", NX, second[:, j * tl : (j + 1) * tl].astype(bf16), -DX[j]) for j in range(1, NX)
    ]
    new_reduce = adam_step(
        cot_slab, activated, w_reduce, reduce_mean, reduce_mean_scale, reduce_var, reduce_var_scale
    )
    in_z_first, in_x_second, new_reduce = hold((in_z_first, in_x_second, new_reduce))
    first = add(pick(first, z), [pick(in_z_first, (z + k) % NZ) for k in range(1, NZ)])
    piece = jnp.concatenate([first, add(second[:, :tl], in_x_second)]).astype(bf16)
    grad_tokens = lax.ppermute(piece, AXES, [(d, s) for s, d in swap_perm()]).T
    return (grad_tokens,) + tuple(new_expand) + tuple(new_reduce)


def solution(mesh):
    four = Mesh(mesh.devices.reshape(NY, NC, NX, NZ), AXES)
    spec = P(("y", "core"), ("x", "z"))
    return jax.shard_map(
        local, mesh=four, in_specs=(spec,) * 12, out_specs=(spec,) * 11, check_vma=False
    )
```
